32 devices in a mesh: space: 16 (over z, x, core), tm: 2 (over y).
Axes of the slice: x: 2, y: 2, z: 4, core: 2. Of those that a mesh axis runs over, the one named last changes fastest.
Arguments:
- node_feats: bfloat16 [128, 7168, 128], P('tm', 'space'), may hold values from -6 to 6
- positions: float32 [128, 3, 7168], P('tm', None, 'space'), may hold values from -3 to 3
- neighbours: int32 [128, 224, 8], P('tm', 'space'), may hold values from 0 to 223, as said below
- edge_in: bfloat16 [256, 128], replicated, may hold values from -0.375 to 0.375
- edge_out: bfloat16 [128, 128], replicated, may hold values from -0.5 to 0.5
- edge_params: float32 [3, 128], replicated, may hold values from -3 to 3
- coord_weight: float32 [128], replicated, may hold values from -0.5 to 0.5
- spectral: bfloat16 [2, 64, 128, 128], replicated, may hold values from -0.375 to 0.375
- node_in: bfloat16 [256, 128], replicated, may hold values from -0.375 to 0.375
- node_out: bfloat16 [128, 128], replicated, may hold values from -0.5 to 0.5
- node_bias: float32 [2, 128], replicated, may hold values from -3 to 3
Outputs:
- new_feats: bfloat16 [128, 7168, 128], P('tm', 'space')
- new_positions: float32 [128, 3, 7168], P('tm', None, 'space')
The draws below stay inside these ranges and needn't reach their ends.
Inputs may be any that keep to these rules, and one draw needn't show every extreme that they name: neighbours[f, b, s] = (b + o) mod 224 for an offset o with -6 <= o <= 6; the offsets of a block's list may repeat, and every list holds the offsets 0, -6 and +6 in some slots.
All inputs are finite; a program needn't handle non-finite values.
Results may differ from the reference program's by a relative error of at most 0.0065.
Values may be sent and summed in bfloat16 or wider, within the bound.
No kernel may reach another device: no remote copies, remote signals or barrier semaphores. Data moves between devices by JAX's collectives and lax.ppermute only.
A program may use at most 320 MiB of HBM per device.

```python
import jax
import jax.numpy as jnp
from jax import lax

H = 128
FRAMES = 128
MODES = 64
NBR = 8
BLOCK = 32
GHOST = 6
P_DEV = 448
PARTICLES = 7168
NBLOCKS = 224


def draw_neighbours(key, part):
    offset_key, order_key = jax.random.split(jax.random.fold_in(key, 17))
    extra_slots = jax.random.randint(offset_key, (FRAMES, NBLOCKS, NBR - 3), -GHOST, GHOST + 1, dtype=jnp.int32)
    fixed_slots = jnp.broadcast_to(jnp.array([0, -GHOST, GHOST], dtype=jnp.int32), (FRAMES, NBLOCKS, 3))
    offsets = jnp.concatenate([fixed_slots, extra_slots], axis=-1)
    scores = jax.random.randint(order_key, (FRAMES, NBLOCKS, NBR), 0, 1 << 20, dtype=jnp.int32) * NBR + jnp.arange(NBR, dtype=jnp.int32)
    ordering = jnp.argsort(scores, axis=-1)
    offsets = jnp.take_along_axis(offsets, ordering, axis=-1)
    block_ids = jnp.arange(NBLOCKS, dtype=jnp.int32)[None, :, None]
    return ((block_ids + offsets) % NBLOCKS).astype(jnp.int32)


def block_scale(own_key, extent, cuts, low, high):
    def one(position, blocks):
        steps = jax.random.uniform(jax.random.fold_in(jax.random.fold_in(own_key, 6), position), (blocks,), jnp.float32, low / len(cuts), high / len(cuts))
        return jnp.repeat(jnp.exp(steps), extent[position] // blocks).reshape((-1,) + (1,) * (len(extent) - position - 1))

    gain = one(*cuts[0])
    for cut in cuts[1:]:
        gain = gain * one(*cut)
    return gain


def gaussian(stream_key, dims, deviation, limit, shards=(), kind=jnp.bfloat16):
    result = deviation * jax.random.normal(stream_key, dims, jnp.float32)
    if shards:
        result = result * block_scale(stream_key, dims, shards, -0.22, 0.18)
    return jnp.clip(result, -limit, limit).astype(kind)


def setup_inputs(seed: int = 0) -> dict:
    seeds = jax.random.split(jax.random.key(seed), 12)
    node_feats = gaussian(seeds[0], (FRAMES, PARTICLES, H), 1.0, 6.0, ((0, 2), (1, 16)))
    positions = gaussian(seeds[1], (FRAMES, 3, PARTICLES), 0.5, 3.0, ((0, 2), (2, 16)), jnp.float32)
    neighbours = draw_neighbours(jax.random.fold_in(seeds[11], 71), 0)
    edge_in = gaussian(seeds[3], (2 * H, H), (2 * H) ** -0.5, 0.375)
    edge_out = gaussian(seeds[4], (H, H), H ** -0.5, 0.5)
    edge_params = gaussian(seeds[5], (3, H), 0.5, 3.0, (), jnp.float32)
    coord_weight = gaussian(seeds[6], (H,), H ** -0.5, 0.5, (), jnp.float32)
    spectral = gaussian(seeds[7], (2, MODES, H, H), (2 * H) ** -0.5, 0.375)
    node_in = gaussian(seeds[8], (2 * H, H), (2 * H) ** -0.5, 0.375)
    node_out = gaussian(seeds[9], (H, H), H ** -0.5, 0.5)
    node_bias = gaussian(seeds[10], (2, H), 0.5, 3.0, (), jnp.float32)
    return dict(node_feats=node_feats, positions=positions, neighbours=neighbours, edge_in=edge_in, edge_out=edge_out, edge_params=edge_params, coord_weight=coord_weight, spectral=spectral, node_in=node_in, node_out=node_out, node_bias=node_bias)


def frame_edges(frame_feats, frame_pos, frame_nbr, edge_in, edge_out, edge_params, coord_weight):
    feat_width = frame_feats.shape[1]
    block_count = frame_nbr.shape[0]
    own_src = jnp.dot(frame_feats, edge_in[:feat_width], preferred_element_type=jnp.float32).reshape(block_count, BLOCK, feat_width)
    all_dst = jnp.dot(frame_feats, edge_in[feat_width:], preferred_element_type=jnp.float32).reshape(block_count, BLOCK, feat_width)
    own_pos = frame_pos.reshape(3, block_count, BLOCK)
    summed = jnp.zeros(own_src.shape, jnp.float32)
    moved = jnp.zeros(own_pos.shape, jnp.float32)
    for slot_num in range(NBR):
        chosen = frame_nbr[:, slot_num]
        near_dst = all_dst[chosen]
        near_pos = own_pos[:, chosen]
        offset_vec = own_pos - near_pos
        dist_sq = lax.optimization_barrier(jnp.sum(offset_vec * offset_vec, axis=0))
        pre_act = own_src + near_dst + edge_params[0] + dist_sq[:, :, None] * edge_params[1]
        hidden = jax.nn.silu(pre_act).astype(jnp.bfloat16)
        out_act = jnp.dot(hidden.reshape(-1, feat_width), edge_out, preferred_element_type=jnp.float32).reshape(pre_act.shape) + edge_params[2]
        message = jax.nn.silu(out_act)
        summed = summed + message
        weight = lax.optimization_barrier(jnp.sum(message * coord_weight, axis=-1)) / (1.0 + jnp.sqrt(dist_sq + 1.0))
        moved = moved + offset_vec * weight[None]
    mean_msg = (summed / NBR).astype(jnp.bfloat16).reshape(-1, feat_width)
    new_pos = frame_pos + (moved / NBR).reshape(3, -1)
    return (mean_msg, new_pos)

def spectral_piece(msg_block, spectral):
    spectrum = jnp.fft.rfft(msg_block.astype(jnp.float32), axis=0)[:MODES]
    real_c = spectrum.real.astype(jnp.bfloat16)
    imag_c = spectrum.imag.astype(jnp.bfloat16)
    real_c, imag_c = lax.optimization_barrier((real_c, imag_c))
    real_c = real_c.astype(jnp.float32)
    imag_c = imag_c.astype(jnp.float32)
    real_w = spectral[0].astype(jnp.float32)
    imag_w = spectral[1].astype(jnp.float32)
    mixed_real = jnp.einsum('knh,khg->kng', real_c, real_w) - jnp.einsum('knh,khg->kng', imag_c, imag_w)
    mixed_imag = jnp.einsum('knh,khg->kng', real_c, imag_w) + jnp.einsum('knh,khg->kng', imag_c, real_w)
    upper = jnp.zeros((FRAMES // 2 + 1 - MODES,) + mixed_real.shape[1:], mixed_real.dtype)
    full_spec = jnp.concatenate([mixed_real, upper], axis=0) + 1j * jnp.concatenate([mixed_imag, upper], axis=0)
    return jnp.fft.irfft(full_spec, n=FRAMES, axis=0).astype(jnp.bfloat16)

def node_update(frame_feats, frame_conv, node_in, node_out, node_bias):
    feat_width = frame_feats.shape[1]
    pre_act = jnp.dot(frame_feats, node_in[:feat_width], preferred_element_type=jnp.float32) + jnp.dot(frame_conv, node_in[feat_width:], preferred_element_type=jnp.float32) + node_bias[0]
    hidden = jax.nn.silu(pre_act).astype(jnp.bfloat16)
    return (frame_feats.astype(jnp.float32) + (jnp.dot(hidden, node_out, preferred_element_type=jnp.float32) + node_bias[1])).astype(jnp.bfloat16)

def reference(node_feats, positions, neighbours, edge_in, edge_out, edge_params, coord_weight, spectral, node_in, node_out, node_bias):

    def per_frame(inputs):
        return frame_edges(inputs[0], inputs[1], inputs[2], edge_in, edge_out, edge_params, coord_weight)
    mean_msg, new_positions = lax.map(per_frame, (node_feats, positions, neighbours))
    piece_count = mean_msg.shape[1] // P_DEV

    def one_piece(piece_num):
        piece = lax.dynamic_slice_in_dim(mean_msg, piece_num * P_DEV, P_DEV, 1)
        return spectral_piece(piece, spectral)
    stacked = lax.map(one_piece, jnp.arange(piece_count, dtype=jnp.int32))
    conv_all = jnp.transpose(stacked, (1, 0, 2, 3)).reshape(FRAMES, -1, mean_msg.shape[2])

    def per_node(inputs):
        return node_update(inputs[0], inputs[1], node_in, node_out, node_bias)
    new_feats = lax.map(per_node, (node_feats, conv_all))
    return (new_feats, new_positions)
```

```python
import functools
import math

import jax
import jax.numpy as jnp
from jax import lax
from jax.experimental import pallas as pl
from jax.experimental.pallas import tpu as pltpu
from jax.sharding import PartitionSpec as P

BLOCK = 32
GHOST = 6
STEP = 8


def silu_half(half):
    return half + half * jnp.tanh(half)


def edge_body(picked, rank, *refs, table, base, first, count, parts, start):
    if table == "own":
        feats, rows, edge_in, edge_out, params, coord = refs[:6]
        rest = refs[6:]
    else:
        feats, rows, halo, edge_in, edge_out, params, coord = refs[:7]
        rest = refs[7:]
    outs, moved = rest[:parts], rest[parts]
    dst, src, near, spots, sums, hid = rest[parts + 1 :]
    width = edge_out.shape[1]
    slots = picked.shape[1] // (feats.shape[1] // BLOCK)
    ghost_rows = GHOST * BLOCK
    step = pl.program_id(0)
    w_src = edge_in[:width] * 0.5
    w_dst = edge_in[width:] * 0.5
    w_out = edge_out[...] * 0.5
    bias_in = params[0:1] * 0.5
    slope = params[1:2] * 0.5
    bias_out = params[2:3] * 0.5
    coord_high = coord[...].astype(jnp.bfloat16)
    coord_low = (coord[...] - coord_high.astype(jnp.float32)).astype(jnp.bfloat16)
    coord_rows = jnp.concatenate(
        [jnp.broadcast_to(coord_high, (slots, width)), jnp.broadcast_to(coord_low, (slots, width))],
        axis=0,
    )
    lane = lax.broadcasted_iota(jnp.int32, (slots, width), 1) // BLOCK
    sub = lax.broadcasted_iota(jnp.int32, (slots, width), 0)
    per = width // BLOCK
    masks = [lane + per * q == sub for q in range(slots // per)]

    def frame(f, carry):
        own_rows = feats.shape[1]
        if table == "low":
            dst[:ghost_rows] = jnp.dot(
                halo[f, :ghost_rows], w_dst, preferred_element_type=jnp.float32
            )
            keep = (first + count + GHOST) * BLOCK
            dst[ghost_rows : ghost_rows + keep] = jnp.dot(
                feats[f, :keep], w_dst, preferred_element_type=jnp.float32
            )
            spots[:8] = halo[f, ghost_rows:].astype(jnp.float32)
            spots[8:24] = rows[f]
            row_of, own_at = 2, 8
        elif table == "high":
            skip = (first - GHOST) * BLOCK
            dst[skip:own_rows] = jnp.dot(
                feats[f, skip:], w_dst, preferred_element_type=jnp.float32
            )
            dst[own_rows : own_rows + ghost_rows] = jnp.dot(
                halo[f, :ghost_rows], w_dst, preferred_element_type=jnp.float32
            )
            spots[:16] = rows[f]
            blocks = own_rows // BLOCK
            spots[blocks : blocks + 8] = halo[f, ghost_rows:].astype(jnp.float32)
            row_of, own_at = 0, 0
        else:
            dst[:own_rows] = jnp.dot(feats[f], w_dst, preferred_element_type=jnp.float32)
            spots[:16] = rows[f]
            row_of, own_at = 0, 0
        src[...] = (
            jnp.dot(
                feats[f, first * BLOCK : (first + count) * BLOCK],
                w_src,
                preferred_element_type=jnp.float32,
            )
            + bias_in
        )
        at = start + step * STEP + f
        for b in range(count):
            chosen = [picked[at, (first + b) * slots + s] - base for s in range(slots)]
            for s in range(slots):
                near[b * slots + s : b * slots + s + 1] = spots[pl.ds(chosen[s] + row_of, 1)]
            here = spots[own_at + first + b : own_at + first + b + 1]
            offset = here - near[b * slots : (b + 1) * slots]
            square = offset * offset
            dist = square + pltpu.roll(square, width // 2, 1)
            dist = dist + pltpu.roll(dist, width // 4, 1)
            gain = offset / (1.0 + jnp.sqrt(dist + 1.0))
            dist_t = jnp.transpose(dist)[:BLOCK]
            own = src[b * BLOCK : (b + 1) * BLOCK]
            for s in range(slots):
                other = dst[pl.ds(pl.multiple_of(chosen[s] * BLOCK, BLOCK), BLOCK)]
                pre = own + other + dist_t[:, s : s + 1] * slope
                hid[b % 2, s * BLOCK : (s + 1) * BLOCK] = silu_half(pre).astype(jnp.bfloat16)
            act = jnp.dot(hid[b % 2], w_out, preferred_element_type=jnp.float32) + bias_out
            message = silu_half(act)
            total = message[:BLOCK]
            for s in range(1, slots):
                total = total + message[s * BLOCK : (s + 1) * BLOCK]
            sums[pl.ds(b * BLOCK * STEP + f, BLOCK, stride=STEP), :] = total
            weight = lax.dot_general(
                coord_rows,
                message.astype(jnp.bfloat16),
                (((1,), (1,)), ((), ())),
                preferred_element_type=jnp.float32,
            )
            weight = weight[:slots] + weight[slots:]
            spread = jnp.zeros((slots, width), jnp.float32)
            for q, mask in enumerate(masks):
                spread = jnp.where(mask, weight[:, q * width : (q + 1) * width], spread)
            spread = spread + pltpu.roll(spread, width // 2, 1)
            spread = spread + pltpu.roll(spread, width // 4, 1)
            moved[f, b : b + 1] = jnp.sum(gain * spread, axis=0, keepdims=True) * (1.0 / slots)
        return carry

    lax.fori_loop(0, STEP, frame, 0)
    share = count * BLOCK // parts
    for r in range(parts):
        part = lax.rem(rank[0] + r, parts)
        block = sums[pl.ds(pl.multiple_of(part * share * STEP, STEP), share * STEP)]
        outs[r][...] = (
            (block * (1.0 / slots)).astype(jnp.bfloat16).reshape(share, STEP, width)
        )


def edge_call(
    rank, picked, feats, rows, halo, weights, *, table, first, count, start, frames, parts
):
    width = feats.shape[2]
    own_rows = feats.shape[1]
    slots = picked.shape[1] // (own_rows // BLOCK)
    shift = start // STEP
    share = count * BLOCK // parts
    ins = [
        pl.BlockSpec((STEP, own_rows, width), lambda i, *_: (i + shift, 0, 0)),
        pl.BlockSpec((STEP,) + rows.shape[1:], lambda i, *_: (i + shift, 0, 0)),
    ]
    args = [feats, rows]
    if halo is not None:
        ins.append(pl.BlockSpec((STEP,) + halo.shape[1:], lambda i, *_: (i, 0, 0)))
        args.append(halo)
    for w in weights:
        ins.append(pl.BlockSpec(w.shape, lambda i, *_: (0, 0)))
    out_shape = [jax.ShapeDtypeStruct((share, frames, width), jnp.bfloat16)] * parts
    out_specs = [pl.BlockSpec((share, STEP, width), lambda i, *_: (0, i, 0))] * parts
    out_shape.append(jax.ShapeDtypeStruct((frames, count, width), jnp.float32))
    out_specs.append(pl.BlockSpec((STEP, count, width), lambda i, *_: (i, 0, 0)))
    edges = frames * count * BLOCK * slots
    base = 0 if table == "low" else GHOST
    return pl.pallas_call(
        functools.partial(
            edge_body, table=table, base=base, first=first, count=count, parts=parts, start=start
        ),
        out_shape=out_shape,
        grid_spec=pltpu.PrefetchScalarGridSpec(
            num_scalar_prefetch=2,
            grid=(frames // STEP,),
            in_specs=ins,
            out_specs=out_specs,
            scratch_shapes=[
                pltpu.VMEM((own_rows + GHOST * BLOCK, width), jnp.float32),
                pltpu.VMEM((count * BLOCK, width), jnp.float32),
                pltpu.VMEM((count * slots, width), jnp.float32),
                pltpu.VMEM((32, width), jnp.float32),
                pltpu.VMEM((count * BLOCK * STEP, width), jnp.float32),
                pltpu.VMEM((2, slots * BLOCK, width), jnp.bfloat16),
            ],
        ),
        cost_estimate=pl.CostEstimate(
            flops=edges * width * width * 16, bytes_accessed=edges * 16, transcendentals=0
        ),
        name=f"edge_{table}",
    )(picked, rank, *args, *weights)


def spectral_body(*refs, pieces, parts):
    data = refs[:pieces]
    fwd, inv, mixer = refs[pieces : pieces + 3]
    outs = refs[pieces + 3 : pieces + 3 + parts]
    coef, mixed = refs[pieces + 3 + parts :]
    items, _, width = data[0].shape
    modes = mixer.shape[1]
    total = 2 * modes
    times = inv.shape[1]
    fwd_high, fwd_low = fwd[0], fwd[1]
    inv_high, inv_low = inv[0], inv[1]

    def forward(n, carry):
        column = jnp.concatenate([d[n] for d in data], axis=0)
        value = jnp.dot(fwd_high, column, preferred_element_type=jnp.float32) + jnp.dot(
            fwd_low, column, preferred_element_type=jnp.float32
        )
        coef[pl.ds(n, total, stride=items), :] = value
        return carry

    lax.fori_loop(0, items, forward, 0, unroll=2)

    def mix(k, carry):
        real = coef[pl.ds(pl.multiple_of(k * items, 8), items)].astype(jnp.bfloat16)
        imag = coef[pl.ds(pl.multiple_of((k + modes) * items, 8), items)].astype(jnp.bfloat16)
        w_real, w_imag = mixer[0, k], mixer[1, k]
        left = jnp.concatenate([real, imag], axis=1)
        right = jnp.concatenate(
            [
                jnp.concatenate([w_real, w_imag], axis=1),
                jnp.concatenate([-w_imag, w_real], axis=1),
            ],
            axis=0,
        )
        value = jnp.dot(left, right, preferred_element_type=jnp.float32)
        mixed[pl.ds(k, items, stride=total), :] = value[:, :width]
        mixed[pl.ds(k + modes, items, stride=total), :] = value[:, width:]
        return carry

    lax.fori_loop(0, modes, mix, 0, unroll=2)

    def backward(n, carry):
        column = mixed[pl.ds(pl.multiple_of(n * total, 8), total)]
        high = column.astype(jnp.bfloat16)
        low = (column - high.astype(jnp.float32)).astype(jnp.bfloat16)
        value = (
            jnp.dot(inv_high, high, preferred_element_type=jnp.float32)
            + jnp.dot(inv_low, high, preferred_element_type=jnp.float32)
            + jnp.dot(inv_high, low, preferred_element_type=jnp.float32)
        )
        coef[pl.ds(n, times, stride=items), :] = value
        return carry

    lax.fori_loop(0, items, backward, 0, unroll=2)
    span = times // parts
    for r in range(parts):
        block = coef[r * span * items : (r + 1) * span * items].astype(jnp.bfloat16)
        outs[r][...] = block.reshape(span, items, width)


def spectral_call(data, fwd, inv, mixer, parts):
    items, _, width = data[0].shape
    times = inv.shape[1]
    total = 2 * mixer.shape[1]
    span = times // parts
    flops = items * width * (4 * total * times + 4 * total * width + 6 * total * times)
    return pl.pallas_call(
        functools.partial(spectral_body, pieces=len(data), parts=parts),
        out_shape=[jax.ShapeDtypeStruct((span, items, width), jnp.bfloat16)] * parts,
        scratch_shapes=[
            pltpu.VMEM((max(total, times) * items, width), jnp.float32),
            pltpu.VMEM((total * items, width), jnp.float32),
        ],
        cost_estimate=pl.CostEstimate(
            flops=flops * 4, bytes_accessed=items * times * width * 4, transcendentals=0
        ),
        name="spectral",
    )(*data, fwd, inv, mixer)


def node_body(spot, *refs):
    feats, conv, node_in, node_out, bias, out = refs[0], refs[1], refs[2], refs[3], refs[4], refs[-1]
    frames, rows, width = feats.shape
    w_in = node_in[...] * 0.5
    first_bias = bias[0:1] * 0.5
    group = max(1, min(frames, 256 // rows))

    def chunk(i, carry):
        pick = pl.ds(pl.multiple_of(i * group, group), group)
        x = feats[pick].reshape(group * rows, width)
        c = conv[pick].reshape(group * rows, width)
        pre = (
            jnp.dot(
                jnp.concatenate([x, c], axis=1), w_in, preferred_element_type=jnp.float32
            )
            + first_bias
        )
        hidden = silu_half(pre).astype(jnp.bfloat16)
        value = x.astype(jnp.float32) + (
            jnp.dot(hidden, node_out[...], preferred_element_type=jnp.float32) + bias[1:2]
        )
        out[pick] = value.astype(jnp.bfloat16).reshape(group, rows, width)
        return carry

    lax.fori_loop(0, frames // group, chunk, 0)


def node_call(spot, feats, conv, weights, buffer, rows):
    frames, particles, width = feats.shape
    items = conv.shape[1]
    ins = [
        pl.BlockSpec((frames, rows, width), lambda i, s: (0, s[0] + i, 0)),
        pl.BlockSpec((frames, rows, width), lambda i, s: (0, i, 0)),
    ]
    for w in weights:
        ins.append(pl.BlockSpec(w.shape, lambda i, s: (0, 0)))
    args = [feats, conv, *weights]
    aliases = {}
    if buffer is not None:
        ins.append(pl.BlockSpec(memory_space=pl.ANY))
        args.append(buffer)
        aliases = {len(args): 0}
    return pl.pallas_call(
        node_body,
        out_shape=jax.ShapeDtypeStruct(feats.shape, jnp.bfloat16),
        grid_spec=pltpu.PrefetchScalarGridSpec(
            num_scalar_prefetch=1,
            grid=(items // rows,),
            in_specs=ins,
            out_specs=pl.BlockSpec((frames, rows, width), lambda i, s: (0, s[0] + i, 0)),
        ),
        input_output_aliases=aliases,
        cost_estimate=pl.CostEstimate(
            flops=frames * items * width * width * 12,
            bytes_accessed=frames * items * width * 6,
            transcendentals=0,
        ),
        name="node",
    )(spot, *args)


def split_parts(values):
    high_part = values.astype(jnp.bfloat16)
    low_part = (values - high_part.astype(jnp.float32)).astype(jnp.bfloat16)
    return jnp.stack([high_part, low_part])


def transforms(rank, parts, frames, modes):
    times = parts * frames
    step_angle = 2.0 * math.pi / times
    local = jnp.arange(frames, dtype=jnp.int32)
    ranks = jnp.arange(parts, dtype=jnp.int32)
    mode_ids = jnp.arange(modes, dtype=jnp.int32)
    from_times = (((rank - ranks) % parts)[:, None] * frames + local).reshape(-1)
    to_times = (((rank + ranks) % parts)[:, None] * frames + local).reshape(-1)
    angles = (mode_ids[:, None] * from_times[None, :] % times).astype(jnp.float32) * step_angle
    forward = jnp.concatenate([jnp.cos(angles), -jnp.sin(angles)], axis=0)
    back = (to_times[:, None] * mode_ids[None, :] % times).astype(jnp.float32) * step_angle
    weights = (jnp.where(mode_ids == 0, 1.0, 2.0) / times).astype(jnp.float32)
    inverse = jnp.concatenate([jnp.cos(back) * weights, -jnp.sin(back) * weights], axis=1)
    return split_parts(forward), split_parts(inverse)


def cut(frames, fractions):
    if frames < 64:
        return [(0, frames)]
    sizes = [frames * a // 64 for a in fractions]
    return [(sum(sizes[:i]), size) for i, size in enumerate(sizes)]


def shards(
    node_feats,
    positions,
    neighbours,
    edge_in,
    edge_out,
    edge_params,
    coord_weight,
    spectral,
    node_in,
    node_out,
    node_bias,
):
    frames, local_rows, width = node_feats.shape
    blocks = local_rows // BLOCK
    rim = GHOST * BLOCK
    parts = lax.axis_size("tm")
    spaces = lax.axis_size("space")
    rank = lax.axis_index("tm").astype(jnp.int32)
    total_blocks = blocks * spaces
    first_block = lax.axis_index("space") * blocks - GHOST
    picked = ((neighbours - first_block) % total_blocks).reshape(frames, -1)
    rows = positions.reshape(frames, 3, blocks, BLOCK).transpose(0, 2, 1, 3)
    rows = rows.reshape(frames, blocks, 3 * BLOCK)
    rows = jnp.pad(rows, ((0, 0), (0, 16 - blocks), (0, width - 3 * BLOCK)))
    ranked = rank.reshape(1)
    weights = (edge_in, edge_out, edge_params, coord_weight.reshape(1, width))

    def ring(shift, count):
        return [(i, (i + shift) % count) for i in range(count)]

    def halo(start, size, low):
        part = slice(start, start + size)
        if low:
            spots = jnp.pad(rows[part, blocks - GHOST : blocks], ((0, 0), (2, 0), (0, 0)))
            block = node_feats[part, local_rows - rim :]
        else:
            spots = jnp.pad(rows[part, :GHOST], ((0, 0), (0, 2), (0, 0)))
            block = node_feats[part, :rim]
        payload = jnp.concatenate([block, spots.astype(jnp.bfloat16)], axis=1)
        return lax.ppermute(payload, "space", ring(1 if low else -1, spaces))

    plans = [("low", 0, GHOST, (16, 24, 24))]
    if blocks > 2 * GHOST:
        plans.insert(0, ("own", GHOST, blocks - 2 * GHOST, (64,)))
    plans.append(("high", blocks - GHOST, GHOST, (32, 32)))
    gathered = []
    moves = {}
    for table, first, count, fractions in plans:
        own, sent, shift_rows = [], [[] for _ in range(1, parts)], []
        for start, size in cut(frames, fractions):
            rim_data = None if table == "own" else halo(start, size, table == "low")
            result = edge_call(
                ranked,
                picked,
                node_feats,
                rows,
                rim_data,
                weights,
                table=table,
                first=first,
                count=count,
                start=start,
                frames=size,
                parts=parts,
            )
            own.append(result[0])
            for r in range(1, parts):
                sent[r - 1].append(lax.ppermute(result[r], "tm", ring(r, parts)))
            shift_rows.append(result[parts])
        gathered.append((first, count, own + [x for group in sent for x in group]))
        moves[first] = jnp.concatenate(shift_rows, axis=0)

    moved = jnp.concatenate([moves[key] for key in sorted(moves)], axis=1)
    moved = moved[:, :, : 3 * BLOCK].reshape(frames, blocks, 3, BLOCK).transpose(0, 2, 1, 3)
    new_positions = positions + moved.reshape(frames, 3, local_rows)

    fwd, inv = transforms(rank, parts, frames, spectral.shape[1])
    node_weights = (node_in, node_out, node_bias)
    buffer = None
    for first, count, data in gathered:
        share = count * BLOCK // parts
        unit = math.gcd(share, BLOCK)
        results = spectral_call(data, fwd, inv, spectral, parts)
        for r in range(parts):
            conv = results[r] if r == 0 else lax.ppermute(results[r], "tm", ring(r, parts))
            source = (rank - r) % parts
            spot = ((first * BLOCK + source * share) // unit).astype(jnp.int32).reshape(1)
            buffer = node_call(spot, node_feats, conv, node_weights, buffer, unit)
    return (buffer, new_positions)


def solution(mesh):
    placed = (
        P("tm", "space", None),
        P("tm", None, "space"),
        P("tm", "space", None),
        P(),
        P(),
        P(),
        P(),
        P(),
        P(),
        P(),
        P(),
    )
    return jax.shard_map(
        shards,
        mesh=mesh,
        in_specs=placed,
        out_specs=(P("tm", "space", None), P("tm", None, "space")),
        check_vma=False,
    )
```
